32 devices in a mesh: pipe: 2 (over core), expert: 16 (over z, y, x).
Axes of the slice: x: 2, y: 2, z: 4, core: 2. Of those that a mesh axis runs over, the one named last changes fastest.
Arguments:
- tokens: bfloat16 [2048, 3584], P('expert'), may hold values from -6 to 6
- expert_ids: int32 [2048, 8], P('expert'), may hold values from 0 to 15, all different within a row; in each aligned block of 128 rows (0 to 127, 128 to 255, ...) at most 80 rows name the same one
- combine_weights: float32 [2048, 8], P('expert'), may hold values from 0.1 to 1
- w_gate: bfloat16 [16, 3584, 2048], P('expert', None, 'pipe'), may hold values from -0.09375 to 0.09375
- w_up: bfloat16 [16, 3584, 2048], P('expert', None, 'pipe'), may hold values from -0.09375 to 0.09375
- w_down: bfloat16 [16, 2048, 3584], P('expert', None, 'pipe'), may hold values from -0.125 to 0.125
Outputs:
- mixture: bfloat16 [2048, 3584], P('expert', 'pipe')
The draws below stay inside these ranges and needn't reach their ends.
Inputs may be any that keep to these rules, and one draw needn't show every extreme that they name: `expert_ids`: each row names 8 different experts. Token t belongs to group t // 128; among the rows of one group no expert is named more than 80 times, and some group names some expert exactly 80 times.
All inputs are finite; a program needn't handle non-finite values.
Results may differ from the reference program's by a relative error of at most 0.0058.
Values may be sent and summed in bfloat16 or wider, within the bound.
A program may use at most 128 MiB of HBM per device.

```python
import math
import jax
import jax.numpy as jnp
import numpy as np
from jax import lax

D = 3584
FF = 2048
TOPK = 8
TOK_DEV = 128
EXPERTS = 16
TOKENS = 2048
CAP = 80
N_EXPERT = 16


def steps_of(key, dims, cuts, smallest, top_value):
    def one(dim, blocks):
        steps = jax.random.uniform(jax.random.fold_in(jax.random.fold_in(key, 6), dim), (blocks,), jnp.float32, smallest / len(cuts), top_value / len(cuts))
        return jnp.repeat(jnp.exp(steps), dims[dim] // blocks).reshape((-1,) + (1,) * (len(dims) - dim - 1))

    factor_of = one(*cuts[0])
    for cut in cuts[1:]:
        factor_of = factor_of * one(*cut)
    return factor_of


def routed_block(rng, own, number, rows, amount, top, most, skew):
    ranking = jax.random.permutation(rng, amount)
    crowded, common = load_shares(amount, rows * top, most, skew, True), load_shares(amount, rows * top, most, skew, False)
    places = jnp.arange(amount)

    def named(sizes, turn):
        used = int((sizes > 0).sum())
        fixed = max(1, used // 4)
        moved = fixed + (places - fixed + turn * (used - fixed)) % max(1, amount - fixed)
        return jnp.zeros((amount,), jnp.int32).at[ranking[jnp.where(places < fixed, places, moved)]].set(jnp.asarray(sizes, jnp.int32))

    sizes = jnp.where(number % 4 == 0, named(crowded, number // 4), named(common, number - number // 4 - 1))
    mixed = jax.random.permutation(jax.random.fold_in(own, 3), amount)
    donor, sink = mixed[0:amount // 2 * 2:2], mixed[1:amount // 2 * 2:2]
    room = jnp.minimum(sizes[donor] - 1, most - sizes[sink]) // 2
    room = jnp.where((donor == ranking[0]) | (sink == ranking[0]) | (sizes[sink] == 0), 0, jnp.maximum(room, 0))
    moved = jax.random.randint(jax.random.fold_in(own, 4), (amount // 2,), 0, 1 << 20) % (room + 1)
    sizes = sizes.at[donor].add(-moved).at[sink].add(moved)
    labels = jnp.searchsorted(jnp.cumsum(sizes), jnp.arange(rows * top), side="right").astype(jnp.int32)
    grid = labels.reshape(top, rows).T
    grid = grid[jax.random.permutation(jax.random.fold_in(own, 1), rows)]
    turn = jax.random.randint(jax.random.fold_in(own, 2), (rows, 1), 0, top)
    return jnp.take_along_axis(grid, (jnp.arange(top)[None, :] + turn) % top, axis=1)


def load_shares(amount, total, bound, lean, full):
    portions = [(1 << 20) // math.isqrt(grade ** lean) + 1 for grade in range(1, amount + 1)]
    largest = bound if full else min(bound, max(-(-total // amount), total * portions[0] // sum(portions)))
    least = 1 if total - largest >= amount - 1 else 0
    given, rest = [largest] + [least] * (amount - 1), total - largest - least * (amount - 1)
    while rest > 0:
        free = [i for i in range(1, amount) if given[i] < largest] or [i for i in range(1, amount) if given[i] < bound]
        mass, remaining = sum([portions[i] for i in free]), rest
        for i in free:
            extra = min(bound - given[i], max(1, remaining * portions[i] // mass), rest)
            given[i] = given[i] + extra
            rest = rest - extra
    return np.array(given)


def scatter_about(key, extent, spread, bound, shards=(), kind=jnp.bfloat16):
    values = spread * jax.random.normal(key, extent, jnp.float32)
    if shards:
        values = values * steps_of(key, extent, shards, -0.22, 0.18)
    return jnp.clip(values, -bound, bound).astype(kind)


def setup_inputs(seed: int = 0) -> dict:
    arg_keys = jax.random.split(jax.random.key(seed), 7)
    tokens = scatter_about(arg_keys[0], (TOKENS, D), 1.0, 6.0, ((0, 16),))
    expert_ids_keys = jax.random.split(jax.random.fold_in(arg_keys[1], 1), TOKENS // TOK_DEV)
    expert_ids_turns = jax.random.permutation(jax.random.fold_in(arg_keys[1], 3), TOKENS // TOK_DEV)
    expert_ids = jax.vmap(lambda own, number: routed_block(jax.random.fold_in(arg_keys[1], 2), own, number, TOK_DEV, EXPERTS, TOPK, CAP, 2))(expert_ids_keys, expert_ids_turns).reshape((TOKENS, TOPK))
    combine_weights = jnp.clip(0.1 + 0.9 * jax.random.uniform(arg_keys[2], (TOKENS, TOPK), jnp.float32) ** steps_of(arg_keys[2], (TOKENS, TOPK), ((0, 16),), -0.2, 0.2), 0.1, 1.0)
    w_gate = scatter_about(arg_keys[3], (EXPERTS, D, FF), D ** -0.5, 0.09375, ((0, 16), (2, 2)))
    w_up = scatter_about(arg_keys[4], (EXPERTS, D, FF), D ** -0.5, 0.09375, ((0, 16), (2, 2)))
    w_down = scatter_about(arg_keys[5], (EXPERTS, FF, D), FF ** -0.5, 0.125, ((0, 16), (2, 2)))
    return dict(tokens=tokens, expert_ids=expert_ids, combine_weights=combine_weights, w_gate=w_gate, w_up=w_up, w_down=w_down)


def reference(tokens, expert_ids, combine_weights, w_gate, w_up, w_down):
    group_count = N_EXPERT
    grouped_ids = expert_ids.reshape(group_count, TOK_DEV, TOPK).astype(jnp.int32)
    expert_iota = jnp.arange(EXPERTS).astype(jnp.int32)
    chosen = (grouped_ids[..., None] == expert_iota).astype(jnp.int32)
    expert_hits = jnp.sum(chosen, axis=2)
    rank_table = jnp.cumsum(expert_hits, axis=1) - expert_hits
    slot_rank = jnp.sum(chosen * rank_table[:, :, None, :], axis=3).astype(jnp.int32)
    group_index = jnp.arange(group_count).astype(jnp.int32)[:, None, None]
    column = (group_index * CAP + slot_rank).astype(jnp.int32)
    token_index = group_index * TOK_DEV + jnp.arange(TOK_DEV).astype(jnp.int32)[None, :, None]
    token_index = jnp.broadcast_to(token_index, grouped_ids.shape).astype(jnp.int32)
    token_table = jnp.full((EXPERTS, group_count * CAP), TOKENS, jnp.int32)
    token_table = token_table.at[grouped_ids, column].set(token_index)
    weight_table = jnp.zeros((EXPERTS, group_count * CAP), jnp.float32)
    weight_table = weight_table.at[grouped_ids, column].set(combine_weights.reshape(group_count, TOK_DEV, TOPK))
    padded = jnp.concatenate([tokens, jnp.zeros((1, D), tokens.dtype)], axis=0)

    def one_expert(running, expert):
        rows_here = token_table[expert]
        gathered = padded[rows_here]
        gate = jnp.dot(gathered, w_gate[expert], preferred_element_type=jnp.float32)
        up_val = jnp.dot(gathered, w_up[expert], preferred_element_type=jnp.float32)
        hidden = (jax.nn.silu(gate) * up_val).astype(jnp.bfloat16)
        expert_out = jnp.dot(hidden, w_down[expert], preferred_element_type=jnp.float32).astype(jnp.bfloat16)
        weighted = weight_table[expert][:, None] * expert_out.astype(jnp.float32)
        return running.at[rows_here].add(weighted), None

    start_acc = jnp.zeros((TOKENS + 1, D), jnp.float32)
    final_acc, unused = lax.scan(one_expert, start_acc, jnp.arange(EXPERTS).astype(jnp.int32))
    return final_acc[:TOKENS].astype(jnp.bfloat16)
```

```python
import jax
import jax.numpy as jnp
from jax import lax
from jax.sharding import PartitionSpec as P


def split_dots(mine, weights):
    place = lax.axis_index("pipe")
    other = lax.ppermute(mine, "pipe", [(0, 1), (1, 0)])
    share = mine.shape[1]
    totals = []
    for weight in weights:
        own = lax.dynamic_slice_in_dim(weight, place * share, share, 0)
        far = lax.dynamic_slice_in_dim(weight, (1 - place) * share, share, 0)
        total = jnp.dot(mine, own, preferred_element_type=jnp.float32)
        totals.append(total + jnp.dot(other, far, preferred_element_type=jnp.float32))
    return totals


def body(tokens, expert_ids, combine_weights, w_gate, w_up, w_down):
    experts = lax.axis_size("expert")
    tok_rows, model_width = tokens.shape
    top_count = expert_ids.shape[1]
    capacity = min(tok_rows, 5 * tok_rows * top_count // (4 * experts))
    slot_count = experts * capacity
    out_width = w_down.shape[2]
    expert_iota = lax.broadcasted_iota(jnp.int32, (1, 1, experts), 2)
    chosen = (expert_ids[:, :, None] == expert_iota).astype(jnp.int32)
    expert_hits = jnp.sum(chosen, axis=1)
    rank_table = jnp.cumsum(expert_hits, axis=0) - expert_hits
    slot_rank = jnp.sum(chosen * rank_table[:, None, :], axis=2)
    target = expert_ids * capacity + slot_rank
    slot_iota = lax.broadcasted_iota(jnp.int32, (1, 1, slot_count), 2)
    slot_marks = target[:, :, None] == slot_iota
    placing = jnp.any(slot_marks, axis=1).astype(jnp.bfloat16)
    blend_table = jnp.sum(jnp.where(slot_marks, combine_weights[:, :, None], 0.0), axis=1)
    pipes = lax.axis_size("pipe")
    place = lax.axis_index("pipe")
    width_share = model_width // pipes
    tok_share = lax.dynamic_slice_in_dim(tokens, place * width_share, width_share, 1)
    packed = jnp.einsum("ts,td->sd", placing, tok_share, preferred_element_type=jnp.float32)
    packed = packed.astype(jnp.bfloat16).reshape(experts, capacity, width_share)
    received = lax.all_to_all(packed, "expert", split_axis=0, concat_axis=0, tiled=True)
    rows = received.reshape(slot_count, width_share)
    if pipes == 2:
        gate_acc, up_acc = split_dots(rows, [w_gate[0], w_up[0]])
    else:
        rows = lax.all_gather(rows, "pipe", axis=1, tiled=True)
        gate_acc = jnp.dot(rows, w_gate[0], preferred_element_type=jnp.float32)
        up_acc = jnp.dot(rows, w_up[0], preferred_element_type=jnp.float32)
    hidden_rows = (jax.nn.silu(gate_acc) * up_acc).astype(jnp.bfloat16)
    if pipes == 2:
        (outputs,) = split_dots(hidden_rows, [w_down[0]])
    else:
        outputs = jnp.dot(
            lax.all_gather(hidden_rows, "pipe", axis=1, tiled=True),
            w_down[0],
            preferred_element_type=jnp.float32,
        )
    outgoing = outputs.astype(jnp.bfloat16).reshape(experts, capacity, out_width)
    returned_rows = lax.all_to_all(outgoing, "expert", split_axis=0, concat_axis=0, tiled=True)
    mixture = jnp.dot(
        blend_table,
        returned_rows.reshape(slot_count, out_width).astype(jnp.float32),
        precision=lax.Precision.HIGHEST,
        preferred_element_type=jnp.float32,
    )
    return mixture.astype(jnp.bfloat16)


def solution(mesh):
    placed = (
        P("expert", None),
        P("expert", None),
        P("expert", None),
        P("expert", None, "pipe"),
        P("expert", None, "pipe"),
        P("expert", None, "pipe"),
    )
    return jax.shard_map(
        body, mesh=mesh, in_specs=placed, out_specs=P("expert", "pipe"), check_vma=False
    )
```

```python
import jax
import jax.numpy as jnp
from jax import lax
from jax.experimental import pallas as pl
from jax.experimental.pallas import tpu as pltpu
from jax.sharding import PartitionSpec as P

LAYERS, SIDE = 4, 2
MESH = pl.DeviceIdType.MESH


def grid_place():
    me = lax.axis_index("expert")
    return me // 4, lax.rem(me // 2, 2), lax.rem(me, 2)


def flat_place(z, y, x):
    return z * 4 + y * 2 + x


def greet():
    z, y, x = grid_place()
    barrier = pltpu.get_barrier_semaphore()
    partners = [flat_place(lax.rem(z + k, LAYERS), y, x) for k in range(1, LAYERS)]
    partners += [flat_place(z, 1 - y, x), flat_place(z, y, 1 - x)]
    for partner in partners:
        pl.semaphore_signal(barrier, inc=1, device_id={"expert": partner}, device_id_type=MESH)
    pl.semaphore_wait(barrier, len(partners))


def gather_kernel(tok_ref, table_ref, out_ref, tables_ref, send_sem, recv_sem, local_sem):
    z, y, x = grid_place()
    me = flat_place(z, y, x)
    greet()
    own = [tok_ref.at[0], tok_ref.at[1], table_ref]
    slots = [lambda e: out_ref.at[e, 0], lambda e: out_ref.at[e, 1], lambda e: tables_ref.at[e]]
    hops = [
        (flat_place(z, 1 - y, x), flat_place(z, y, 1 - x)),
        (flat_place(z, y, 1 - x), flat_place(z, 1 - y, x)),
        (flat_place(z, 1 - y, x), flat_place(z, y, 1 - x)),
    ]
    kept = [pltpu.make_async_copy(own[j], slots[j](me), local_sem.at[j]) for j in range(3)]
    started = []

    def send(source, slot, partner, j, k, step):
        copy = pltpu.make_async_remote_copy(
            src_ref=source, dst_ref=slot, send_sem=send_sem.at[j, k, step],
            recv_sem=recv_sem.at[j, k, step], device_id={"expert": partner}, device_id_type=MESH,
        )
        copy.start()
        started.append(copy)
        return copy

    order = (2, 0, 1)
    along = {}
    for k in range(1, LAYERS):
        for j in order:
            along[j, k] = send(own[j], slots[j](me), flat_place(lax.rem(z + k, LAYERS), y, x), j, k, 0)
    near = {}

    def spread(k):
        origin = flat_place(lax.rem(z - k + LAYERS, LAYERS), y, x)
        for j in order:
            if k:
                along[j, k].wait_recv()
            source = slots[j](origin) if k else own[j]
            near[j, k] = send(source, slots[j](origin), hops[j][0], j, k, 1)
            send(source, slots[j](origin), hops[j][1], j, k, 2)

    def forward(k):
        layer = lax.rem(z - k + LAYERS, LAYERS)
        for j in order:
            origin = flat_place(layer, y, 1 - x) if j == 1 else flat_place(layer, 1 - y, x)
            near[j, k].wait_recv()
            send(slots[j](origin), slots[j](origin), hops[j][1], j, k, 3)

    spread(0)
    for copy in kept:
        copy.start()
    for k in range(1, LAYERS):
        spread(k)
        forward(k - 1)
    forward(LAYERS - 1)
    for copy in kept:
        copy.wait()
    for copy in started:
        copy.wait_send()
    waited = list(along.values()) + list(near.values())
    for copy in started:
        if not any(copy is other for other in waited):
            copy.wait_recv()


def gather_rows(tokens, table):
    rows, width = tokens.shape
    experts = lax.axis_size("expert")
    half = rows // 2
    anywhere = pl.BlockSpec(memory_space=pl.ANY)
    gathered, tables = pl.pallas_call(
        gather_kernel,
        out_shape=(
            jax.ShapeDtypeStruct((experts, 2, half, width), tokens.dtype),
            jax.ShapeDtypeStruct((experts, rows, table.shape[1]), table.dtype),
        ),
        in_specs=[anywhere, anywhere],
        out_specs=(anywhere, anywhere),
        scratch_shapes=[
            pltpu.SemaphoreType.DMA((3, LAYERS, 4)),
            pltpu.SemaphoreType.DMA((3, LAYERS, 4)),
            pltpu.SemaphoreType.DMA((3,)),
        ],
        compiler_params=pltpu.CompilerParams(collective_id=0, has_side_effects=True),
    )(tokens.reshape(2, half, width), table)
    return gathered.reshape(experts, rows, width), tables


def reduce_kernel(part_ref, out_ref, first, second, last, send1, recv1, send2, recv2, send3, recv3):
    z, y, x = grid_place()
    greet()

    def target(k, h, far_first, far_second):
        layer = lax.rem(z + k, LAYERS)
        flip_y, flip_x = (far_second, far_first) if h == 0 else (far_first, far_second)
        return flat_place(layer, 1 - y if flip_y else y, 1 - x if flip_x else x)

    def send(source, slot, partner, send_sem, recv_sem):
        copy = pltpu.make_async_remote_copy(
            src_ref=source, dst_ref=slot, send_sem=send_sem, recv_sem=recv_sem,
            device_id={"expert": partner}, device_id_type=MESH,
        )
        copy.start()
        return copy

    wide = jnp.float32
    order = (2, 1, 3, 0)
    one, two, three = {}, {}, {}
    for k in order:
        for j in range(2):
            for h in range(2):
                one[h, k, j] = send(
                    part_ref.at[target(k, h, True, j == 0), h], first.at[h, k, j],
                    target(0, h, True, False), send1.at[h, k, j], recv1.at[h, k, j],
                )

    def pass_on(k):
        for h in range(2):
            one[h, k, 0].wait_recv()
            mine = part_ref[target(k, h, False, True), h].astype(wide)
            first[h, k, 0] = (mine + first[h, k, 0].astype(wide)).astype(first.dtype)
            two[h, k] = send(
                first.at[h, k, 0], second.at[h, k], target(0, h, False, True),
                send2.at[h, k], recv2.at[h, k],
            )

    def total(k, h):
        one[h, k, 1].wait_recv()
        two[h, k].wait_recv()
        mine = part_ref[target(k, h, False, False), h].astype(wide)
        return mine + first[h, k, 1].astype(wide) + second[h, k].astype(wide)

    def climb(k):
        for h in range(2):
            second[h, k] = total(k, h).astype(second.dtype)
            three[h, k] = send(
                second.at[h, k], last.at[h, k - 1], target(k, h, False, False),
                send3.at[h, k - 1], recv3.at[h, k - 1],
            )

    pass_on(order[0])
    for before, k in zip(order[:-1], order[1:]):
        pass_on(k)
        climb(before)
    for h in range(2):
        value = total(0, h)
        for k in order[:-1]:
            three[h, k].wait_recv()
            value = value + last[h, k - 1].astype(wide)
        out_ref[h] = value.astype(out_ref.dtype)
    for copy in list(one.values()) + list(two.values()) + list(three.values()):
        copy.wait_send()


def reduce_rows(parts):
    experts, rows, width = parts.shape
    half = rows // 2
    inside = pl.BlockSpec(memory_space=pltpu.VMEM)
    dma = pltpu.SemaphoreType.DMA
    mixed = pl.pallas_call(
        reduce_kernel,
        out_shape=jax.ShapeDtypeStruct((2, half, width), parts.dtype),
        in_specs=[inside],
        out_specs=inside,
        scratch_shapes=[
            pltpu.VMEM((2, LAYERS, 2, half, width), parts.dtype),
            pltpu.VMEM((2, LAYERS, half, width), parts.dtype),
            pltpu.VMEM((2, LAYERS - 1, half, width), parts.dtype),
            dma((2, LAYERS, 2)), dma((2, LAYERS, 2)),
            dma((2, LAYERS)), dma((2, LAYERS)),
            dma((2, LAYERS - 1)), dma((2, LAYERS - 1)),
        ],
        compiler_params=pltpu.CompilerParams(
            collective_id=1, has_side_effects=True, vmem_limit_bytes=40 * 1024 * 1024
        ),
    )(parts.reshape(experts, 2, half, width))
    return mixed.reshape(rows, width)


def tree_body(tokens, expert_ids, combine_weights, w_gate, w_up, w_down):
    experts = lax.axis_size("expert")
    tok_rows, model_width = tokens.shape
    top_count = expert_ids.shape[1]
    capacity = min(tok_rows, 5 * tok_rows * top_count // (4 * experts))
    slot_count = experts * capacity
    out_width = w_down.shape[2]
    width_share = model_width // SIDE
    lanes = 128
    expert_iota = lax.broadcasted_iota(jnp.int32, (1, 1, lanes), 2)
    chosen = expert_ids[:, :, None] == expert_iota
    table = jnp.sum(jnp.where(chosen, combine_weights[:, :, None], 0.0), axis=1)
    place = lax.axis_index("pipe")
    tok_share = lax.dynamic_slice_in_dim(tokens, place * width_share, width_share, 1)
    gathered, tables = gather_rows(tok_share, table)
    mine = lax.broadcasted_iota(jnp.int32, (1, 1, lanes), 2) == lax.axis_index("expert")
    weights = jnp.sum(jnp.where(mine, tables, 0.0), axis=2)
    named = weights > 0.0
    before = lax.broadcasted_iota(jnp.int32, (tok_rows, tok_rows), 0)
    before = before < lax.broadcasted_iota(jnp.int32, (tok_rows, tok_rows), 1)
    rank = jnp.dot(named.astype(jnp.bfloat16), before.astype(jnp.bfloat16), preferred_element_type=jnp.float32)
    slot = jnp.where(named, rank.astype(jnp.int32), -1)
    marks = slot[:, None, :] == lax.broadcasted_iota(jnp.int32, (1, capacity, 1), 1)
    row_weight = jnp.sum(jnp.where(marks, weights[:, None, :], 0.0), axis=2)
    marks = marks.astype(jnp.bfloat16)
    rows = jnp.einsum("gct,gtd->gcd", marks, gathered, preferred_element_type=jnp.float32)
    rows = rows.astype(jnp.bfloat16).reshape(slot_count, width_share)
    gate_acc, up_acc = split_dots(rows, [w_gate[0], w_up[0]])
    hidden_rows = (jax.nn.silu(gate_acc) * up_acc).astype(jnp.bfloat16)
    (outputs,) = split_dots(hidden_rows, [w_down[0]])
    outputs = (outputs * row_weight.reshape(slot_count, 1)).astype(jnp.bfloat16)
    outputs = outputs.reshape(experts, capacity, out_width)
    parts = jnp.einsum("gct,gcd->gtd", marks, outputs, preferred_element_type=jnp.float32)
    return reduce_rows(parts.astype(jnp.bfloat16))


def split_dots(mine, weights):
    place = lax.axis_index("pipe")
    other = lax.ppermute(mine, "pipe", [(0, 1), (1, 0)])
    share = mine.shape[1]
    totals = []
    for weight in weights:
        own = lax.dynamic_slice_in_dim(weight, place * share, share, 0)
        far = lax.dynamic_slice_in_dim(weight, (1 - place) * share, share, 0)
        total = jnp.dot(mine, own, preferred_element_type=jnp.float32)
        totals.append(total + jnp.dot(other, far, preferred_element_type=jnp.float32))
    return totals


def body(tokens, expert_ids, combine_weights, w_gate, w_up, w_down):
    experts = lax.axis_size("expert")
    tok_rows, model_width = tokens.shape
    top_count = expert_ids.shape[1]
    capacity = min(tok_rows, 5 * tok_rows * top_count // (4 * experts))
    slot_count = experts * capacity
    out_width = w_down.shape[2]
    expert_iota = lax.broadcasted_iota(jnp.int32, (1, 1, experts), 2)
    chosen = (expert_ids[:, :, None] == expert_iota).astype(jnp.int32)
    expert_hits = jnp.sum(chosen, axis=1)
    rank_table = jnp.cumsum(expert_hits, axis=0) - expert_hits
    slot_rank = jnp.sum(chosen * rank_table[:, None, :], axis=2)
    target = expert_ids * capacity + slot_rank
    slot_iota = lax.broadcasted_iota(jnp.int32, (1, 1, slot_count), 2)
    slot_marks = target[:, :, None] == slot_iota
    placing = jnp.any(slot_marks, axis=1).astype(jnp.bfloat16)
    blend_table = jnp.sum(jnp.where(slot_marks, combine_weights[:, :, None], 0.0), axis=1)
    pipes = lax.axis_size("pipe")
    place = lax.axis_index("pipe")
    width_share = model_width // pipes
    tok_share = lax.dynamic_slice_in_dim(tokens, place * width_share, width_share, 1)
    packed = jnp.einsum("ts,td->sd", placing, tok_share, preferred_element_type=jnp.float32)
    packed = packed.astype(jnp.bfloat16).reshape(experts, capacity, width_share)
    received = lax.all_to_all(packed, "expert", split_axis=0, concat_axis=0, tiled=True)
    rows = received.reshape(slot_count, width_share)
    if pipes == 2:
        gate_acc, up_acc = split_dots(rows, [w_gate[0], w_up[0]])
    else:
        rows = lax.all_gather(rows, "pipe", axis=1, tiled=True)
        gate_acc = jnp.dot(rows, w_gate[0], preferred_element_type=jnp.float32)
        up_acc = jnp.dot(rows, w_up[0], preferred_element_type=jnp.float32)
    hidden_rows = (jax.nn.silu(gate_acc) * up_acc).astype(jnp.bfloat16)
    if pipes == 2:
        (outputs,) = split_dots(hidden_rows, [w_down[0]])
    else:
        outputs = jnp.dot(
            lax.all_gather(hidden_rows, "pipe", axis=1, tiled=True),
            w_down[0],
            preferred_element_type=jnp.float32,
        )
    outgoing = outputs.astype(jnp.bfloat16).reshape(experts, capacity, out_width)
    returned_rows = lax.all_to_all(outgoing, "expert", split_axis=0, concat_axis=0, tiled=True)
    mixture = jnp.dot(
        blend_table,
        returned_rows.reshape(slot_count, out_width).astype(jnp.float32),
        precision=lax.Precision.HIGHEST,
        preferred_element_type=jnp.float32,
    )
    return mixture.astype(jnp.bfloat16)


def solution(mesh):
    placed = (
        P("expert", None),
        P("expert", None),
        P("expert", None),
        P("expert", None, "pipe"),
        P("expert", None, "pipe"),
        P("expert", None, "pipe"),
    )
    tree = mesh.shape["pipe"] == SIDE and mesh.shape["expert"] == LAYERS * SIDE * SIDE
    return jax.shard_map(
        tree_body if tree else body, mesh=mesh, in_specs=placed, out_specs=P("expert", "pipe"), check_vma=False
    )
```

```python
import jax
import jax.numpy as jnp
from jax import lax
from jax.experimental import pallas as pl
from jax.experimental.pallas import tpu as pltpu
from jax.sharding import PartitionSpec as P

LAYERS, SIDE = 4, 2
MESH = pl.DeviceIdType.MESH


def grid_place():
    me = lax.axis_index("expert")
    return me // 4, lax.rem(me // 2, 2), lax.rem(me, 2)


def flat_place(z, y, x):
    return z * 4 + y * 2 + x


def greet():
    z, y, x = grid_place()
    barrier = pltpu.get_barrier_semaphore()
    partners = [flat_place(lax.rem(z + k, LAYERS), y, x) for k in range(1, LAYERS)]
    partners += [flat_place(z, 1 - y, x), flat_place(z, y, 1 - x)]
    for partner in partners:
        pl.semaphore_signal(barrier, inc=1, device_id={"expert": partner}, device_id_type=MESH)
    pl.semaphore_wait(barrier, len(partners))


def gather_kernel(tok_ref, table_ref, out_ref, tables_ref, send_sem, recv_sem, local_sem):
    z, y, x = grid_place()
    me = flat_place(z, y, x)
    greet()
    own = [tok_ref.at[0], tok_ref.at[1], table_ref]
    slots = [lambda e: out_ref.at[e, 0], lambda e: out_ref.at[e, 1], lambda e: tables_ref.at[e]]
    hops = [
        (flat_place(z, 1 - y, x), flat_place(z, y, 1 - x)),
        (flat_place(z, y, 1 - x), flat_place(z, 1 - y, x)),
        (flat_place(z, 1 - y, x), flat_place(z, y, 1 - x)),
    ]
    kept = [pltpu.make_async_copy(own[j], slots[j](me), local_sem.at[j]) for j in range(3)]
    started = []

    def send(source, slot, partner, j, k, step):
        copy = pltpu.make_async_remote_copy(
            src_ref=source, dst_ref=slot, send_sem=send_sem.at[j, k, step],
            recv_sem=recv_sem.at[j, k, step], device_id={"expert": partner}, device_id_type=MESH,
        )
        copy.start()
        started.append(copy)
        return copy

    order = (2, 0, 1)
    along, near = {}, {}

    def climb(k):
        for j in order:
            along[j, k] = send(own[j], slots[j](me), flat_place(lax.rem(z + k, LAYERS), y, x), j, k, 0)

    def spread(k):
        origin = flat_place(lax.rem(z - k + LAYERS, LAYERS), y, x)
        for j in order:
            source = slots[j](origin) if k else own[j]
            near[j, k] = send(source, slots[j](origin), hops[j][0], j, k, 1)
            send(source, slots[j](origin), hops[j][1], j, k, 2)

    def forward(k):
        layer = lax.rem(z - k + LAYERS, LAYERS)
        for j in order:
            origin = flat_place(layer, y, 1 - x) if j == 1 else flat_place(layer, 1 - y, x)
            near[j, k].wait_recv()
            send(slots[j](origin), slots[j](origin), hops[j][1], j, k, 3)

    climb(1)
    spread(0)
    for copy in kept:
        copy.start()
    previous = 0
    for k, later in ((1, 3), (3, 2), (2, None)):
        for j in order:
            along[j, k].wait_recv()
        if later:
            climb(later)
        spread(k)
        forward(previous)
        previous = k
    forward(previous)
    for copy in kept:
        copy.wait()
    for copy in started:
        copy.wait_send()
    waited = list(along.values()) + list(near.values())
    for copy in started:
        if not any(copy is other for other in waited):
            copy.wait_recv()


def gather_rows(tokens, table):
    rows, width = tokens.shape
    experts = lax.axis_size("expert")
    half = rows // 2
    anywhere = pl.BlockSpec(memory_space=pl.ANY)
    gathered, tables = pl.pallas_call(
        gather_kernel,
        out_shape=(
            jax.ShapeDtypeStruct((experts, 2, half, width), tokens.dtype),
            jax.ShapeDtypeStruct((experts, rows, table.shape[1]), table.dtype),
        ),
        in_specs=[anywhere, anywhere],
        out_specs=(anywhere, anywhere),
        scratch_shapes=[
            pltpu.SemaphoreType.DMA((3, LAYERS, 4)),
            pltpu.SemaphoreType.DMA((3, LAYERS, 4)),
            pltpu.SemaphoreType.DMA((3,)),
        ],
        compiler_params=pltpu.CompilerParams(collective_id=0, has_side_effects=True),
    )(tokens.reshape(2, half, width), table)
    return gathered.reshape(experts, rows, width), tables


def reduce_kernel(part_ref, out_ref, first, second, last, send1, recv1, send2, recv2, send3, recv3):
    z, y, x = grid_place()
    greet()

    def target(k, h, far_first, far_second):
        layer = lax.rem(z + k, LAYERS)
        flip_y, flip_x = (far_second, far_first) if h == 0 else (far_first, far_second)
        return flat_place(layer, 1 - y if flip_y else y, 1 - x if flip_x else x)

    def send(source, slot, partner, send_sem, recv_sem):
        copy = pltpu.make_async_remote_copy(
            src_ref=source, dst_ref=slot, send_sem=send_sem, recv_sem=recv_sem,
            device_id={"expert": partner}, device_id_type=MESH,
        )
        copy.start()
        return copy

    wide = jnp.float32
    order = (2, 1, 3, 0)
    one, two, three = {}, {}, {}

    def open_layer(k):
        for j in range(2):
            for h in range(2):
                one[h, k, j] = send(
                    part_ref.at[target(k, h, True, j == 0), h], first.at[h, k, j],
                    target(0, h, True, False), send1.at[h, k, j], recv1.at[h, k, j],
                )

    def pass_on(k):
        for h in range(2):
            one[h, k, 0].wait_recv()
            mine = part_ref[target(k, h, False, True), h].astype(wide)
            first[h, k, 0] = (mine + first[h, k, 0].astype(wide)).astype(first.dtype)
            two[h, k] = send(
                first.at[h, k, 0], second.at[h, k], target(0, h, False, True),
                send2.at[h, k], recv2.at[h, k],
            )

    def total(k, h):
        one[h, k, 1].wait_recv()
        two[h, k].wait_recv()
        mine = part_ref[target(k, h, False, False), h].astype(wide)
        return mine + first[h, k, 1].astype(wide) + second[h, k].astype(wide)

    def climb(k):
        for h in range(2):
            second[h, k] = total(k, h).astype(second.dtype)
            three[h, k] = send(
                second.at[h, k], last.at[h, k - 1], target(k, h, False, False),
                send3.at[h, k - 1], recv3.at[h, k - 1],
            )

    open_layer(order[0])
    open_layer(order[1])
    pass_on(order[0])
    open_layer(order[2])
    pass_on(order[1])
    climb(order[0])
    open_layer(order[3])
    pass_on(order[2])
    climb(order[1])
    pass_on(order[3])
    climb(order[2])
    for h in range(2):
        value = total(0, h)
        for k in order[:-1]:
            three[h, k].wait_recv()
            value = value + last[h, k - 1].astype(wide)
        out_ref[h] = value.astype(out_ref.dtype)
    for copy in list(one.values()) + list(two.values()) + list(three.values()):
        copy.wait_send()


def reduce_rows(parts):
    experts, rows, width = parts.shape
    half = rows // 2
    inside = pl.BlockSpec(memory_space=pltpu.VMEM)
    dma = pltpu.SemaphoreType.DMA
    mixed = pl.pallas_call(
        reduce_kernel,
        out_shape=jax.ShapeDtypeStruct((2, half, width), parts.dtype),
        in_specs=[inside],
        out_specs=inside,
        scratch_shapes=[
            pltpu.VMEM((2, LAYERS, 2, half, width), parts.dtype),
            pltpu.VMEM((2, LAYERS, half, width), parts.dtype),
            pltpu.VMEM((2, LAYERS - 1, half, width), parts.dtype),
            dma((2, LAYERS, 2)), dma((2, LAYERS, 2)),
            dma((2, LAYERS)), dma((2, LAYERS)),
            dma((2, LAYERS - 1)), dma((2, LAYERS - 1)),
        ],
        compiler_params=pltpu.CompilerParams(
            collective_id=1, has_side_effects=True, vmem_limit_bytes=40 * 1024 * 1024
        ),
    )(parts.reshape(experts, 2, half, width))
    return mixed.reshape(rows, width)


def tree_body(tokens, expert_ids, combine_weights, w_gate, w_up, w_down):
    experts = lax.axis_size("expert")
    tok_rows, model_width = tokens.shape
    top_count = expert_ids.shape[1]
    capacity = min(tok_rows, 5 * tok_rows * top_count // (4 * experts))
    slot_count = experts * capacity
    out_width = w_down.shape[2]
    width_share = model_width // SIDE
    lanes = 128
    expert_iota = lax.broadcasted_iota(jnp.int32, (1, 1, lanes), 2)
    chosen = expert_ids[:, :, None] == expert_iota
    table = jnp.sum(jnp.where(chosen, combine_weights[:, :, None], 0.0), axis=1)
    place = lax.axis_index("pipe")
    tok_share = lax.dynamic_slice_in_dim(tokens, place * width_share, width_share, 1)
    gathered, tables = gather_rows(tok_share, table)
    mine = lax.broadcasted_iota(jnp.int32, (1, 1, lanes), 2) == lax.axis_index("expert")
    weights = jnp.sum(jnp.where(mine, tables, 0.0), axis=2)
    named = weights > 0.0
    before = lax.broadcasted_iota(jnp.int32, (tok_rows, tok_rows), 0)
    before = before < lax.broadcasted_iota(jnp.int32, (tok_rows, tok_rows), 1)
    rank = jnp.dot(named.astype(jnp.bfloat16), before.astype(jnp.bfloat16), preferred_element_type=jnp.float32)
    slot = jnp.where(named, rank.astype(jnp.int32), -1)
    marks = slot[:, None, :] == lax.broadcasted_iota(jnp.int32, (1, capacity, 1), 1)
    row_weight = jnp.sum(jnp.where(marks, weights[:, None, :], 0.0), axis=2)
    marks = marks.astype(jnp.bfloat16)
    rows = jnp.einsum("gct,gtd->gcd", marks, gathered, preferred_element_type=jnp.float32)
    rows = rows.astype(jnp.bfloat16).reshape(slot_count, width_share)
    gate_acc, up_acc = split_dots(rows, [w_gate[0], w_up[0]])
    hidden_rows = (jax.nn.silu(gate_acc) * up_acc).astype(jnp.bfloat16)
    (outputs,) = split_dots(hidden_rows, [w_down[0]])
    outputs = (outputs * row_weight.reshape(slot_count, 1)).astype(jnp.bfloat16)
    outputs = outputs.reshape(experts, capacity, out_width)
    parts = jnp.einsum("gct,gcd->gtd", marks, outputs, preferred_element_type=jnp.float32)
    return reduce_rows(parts.astype(jnp.bfloat16))


def split_dots(mine, weights):
    place = lax.axis_index("pipe")
    other = lax.ppermute(mine, "pipe", [(0, 1), (1, 0)])
    share = mine.shape[1]
    totals = []
    for weight in weights:
        own = lax.dynamic_slice_in_dim(weight, place * share, share, 0)
        far = lax.dynamic_slice_in_dim(weight, (1 - place) * share, share, 0)
        total = jnp.dot(mine, own, preferred_element_type=jnp.float32)
        totals.append(total + jnp.dot(other, far, preferred_element_type=jnp.float32))
    return totals


def body(tokens, expert_ids, combine_weights, w_gate, w_up, w_down):
    experts = lax.axis_size("expert")
    tok_rows, model_width = tokens.shape
    top_count = expert_ids.shape[1]
    capacity = min(tok_rows, 5 * tok_rows * top_count // (4 * experts))
    slot_count = experts * capacity
    out_width = w_down.shape[2]
    expert_iota = lax.broadcasted_iota(jnp.int32, (1, 1, experts), 2)
    chosen = (expert_ids[:, :, None] == expert_iota).astype(jnp.int32)
    expert_hits = jnp.sum(chosen, axis=1)
    rank_table = jnp.cumsum(expert_hits, axis=0) - expert_hits
    slot_rank = jnp.sum(chosen * rank_table[:, None, :], axis=2)
    target = expert_ids * capacity + slot_rank
    slot_iota = lax.broadcasted_iota(jnp.int32, (1, 1, slot_count), 2)
    slot_marks = target[:, :, None] == slot_iota
    placing = jnp.any(slot_marks, axis=1).astype(jnp.bfloat16)
    blend_table = jnp.sum(jnp.where(slot_marks, combine_weights[:, :, None], 0.0), axis=1)
    pipes = lax.axis_size("pipe")
    place = lax.axis_index("pipe")
    width_share = model_width // pipes
    tok_share = lax.dynamic_slice_in_dim(tokens, place * width_share, width_share, 1)
    packed = jnp.einsum("ts,td->sd", placing, tok_share, preferred_element_type=jnp.float32)
    packed = packed.astype(jnp.bfloat16).reshape(experts, capacity, width_share)
    received = lax.all_to_all(packed, "expert", split_axis=0, concat_axis=0, tiled=True)
    rows = received.reshape(slot_count, width_share)
    if pipes == 2:
        gate_acc, up_acc = split_dots(rows, [w_gate[0], w_up[0]])
    else:
        rows = lax.all_gather(rows, "pipe", axis=1, tiled=True)
        gate_acc = jnp.dot(rows, w_gate[0], preferred_element_type=jnp.float32)
        up_acc = jnp.dot(rows, w_up[0], preferred_element_type=jnp.float32)
    hidden_rows = (jax.nn.silu(gate_acc) * up_acc).astype(jnp.bfloat16)
    if pipes == 2:
        (outputs,) = split_dots(hidden_rows, [w_down[0]])
    else:
        outputs = jnp.dot(
            lax.all_gather(hidden_rows, "pipe", axis=1, tiled=True),
            w_down[0],
            preferred_element_type=jnp.float32,
        )
    outgoing = outputs.astype(jnp.bfloat16).reshape(experts, capacity, out_width)
    returned_rows = lax.all_to_all(outgoing, "expert", split_axis=0, concat_axis=0, tiled=True)
    mixture = jnp.dot(
        blend_table,
        returned_rows.reshape(slot_count, out_width).astype(jnp.float32),
        precision=lax.Precision.HIGHEST,
        preferred_element_type=jnp.float32,
    )
    return mixture.astype(jnp.bfloat16)


def solution(mesh):
    placed = (
        P("expert", None),
        P("expert", None),
        P("expert", None),
        P("expert", None, "pipe"),
        P("expert", None, "pipe"),
        P("expert", None, "pipe"),
    )
    tree = mesh.shape["pipe"] == SIDE and mesh.shape["expert"] == LAYERS * SIDE * SIDE
    return jax.shard_map(
        tree_body if tree else body, mesh=mesh, in_specs=placed, out_specs=P("expert", "pipe"), check_vma=False
    )
```

```python
import jax
import jax.numpy as jnp
from jax import lax
from jax.experimental import pallas as pl
from jax.experimental.pallas import tpu as pltpu
from jax.sharding import PartitionSpec as P

LAYERS, SIDE = 4, 2
MESH = pl.DeviceIdType.MESH


def grid_place():
    me = lax.axis_index("expert")
    return me // 4, lax.rem(me // 2, 2), lax.rem(me, 2)


def flat_place(z, y, x):
    return z * 4 + y * 2 + x


def greet():
    z, y, x = grid_place()
    barrier = pltpu.get_barrier_semaphore()
    partners = [flat_place(lax.rem(z + k, LAYERS), y, x) for k in range(1, LAYERS)]
    partners += [flat_place(z, 1 - y, x), flat_place(z, y, 1 - x)]
    for partner in partners:
        pl.semaphore_signal(barrier, inc=1, device_id={"expert": partner}, device_id_type=MESH)
    pl.semaphore_wait(barrier, len(partners))


def gather_kernel(tok_ref, table_ref, out_ref, tables_ref, send_sem, recv_sem, local_sem):
    z, y, x = grid_place()
    me = flat_place(z, y, x)
    greet()
    own = [tok_ref.at[0], tok_ref.at[1], table_ref]
    slots = [lambda e: out_ref.at[e, 0], lambda e: out_ref.at[e, 1], lambda e: tables_ref.at[e]]
    hops = [
        (flat_place(z, 1 - y, x), flat_place(z, y, 1 - x)),
        (flat_place(z, y, 1 - x), flat_place(z, 1 - y, x)),
        (flat_place(z, 1 - y, x), flat_place(z, y, 1 - x)),
    ]
    kept = [pltpu.make_async_copy(own[j], slots[j](me), local_sem.at[j]) for j in range(3)]
    started = []

    def send(source, slot, partner, j, k, step):
        copy = pltpu.make_async_remote_copy(
            src_ref=source, dst_ref=slot, send_sem=send_sem.at[j, k, step],
            recv_sem=recv_sem.at[j, k, step], device_id={"expert": partner}, device_id_type=MESH,
        )
        copy.start()
        started.append(copy)
        return copy

    order = (2, 0, 1)
    along, near = {}, {}

    def climb(k):
        for j in order:
            along[j, k] = send(own[j], slots[j](me), flat_place(lax.rem(z + k, LAYERS), y, x), j, k, 0)

    def spread(k):
        origin = flat_place(lax.rem(z - k + LAYERS, LAYERS), y, x)
        for j in order:
            source = slots[j](origin) if k else own[j]
            near[j, k] = send(source, slots[j](origin), hops[j][0], j, k, 1)
            send(source, slots[j](origin), hops[j][1], j, k, 2)

    def forward(k):
        layer = lax.rem(z - k + LAYERS, LAYERS)
        for j in order:
            origin = flat_place(layer, y, 1 - x) if j == 1 else flat_place(layer, 1 - y, x)
            near[j, k].wait_recv()
            send(slots[j](origin), slots[j](origin), hops[j][1], j, k, 3)

    climb(1)
    spread(0)
    for copy in kept:
        copy.start()
    previous = 0
    for k, later in ((1, 3), (3, 2), (2, None)):
        for j in order:
            along[j, k].wait_recv()
        if later:
            climb(later)
        spread(k)
        forward(previous)
        previous = k
    forward(previous)
    for copy in kept:
        copy.wait()
    for copy in started:
        copy.wait_send()
    waited = list(along.values()) + list(near.values())
    for copy in started:
        if not any(copy is other for other in waited):
            copy.wait_recv()


def gather_rows(tokens, table):
    rows, width = tokens.shape
    experts = lax.axis_size("expert")
    half = rows // 2
    anywhere = pl.BlockSpec(memory_space=pl.ANY)
    gathered, tables = pl.pallas_call(
        gather_kernel,
        out_shape=(
            jax.ShapeDtypeStruct((experts, 2, half, width), tokens.dtype),
            jax.ShapeDtypeStruct((experts,) + table.shape, table.dtype),
        ),
        in_specs=[anywhere, anywhere],
        out_specs=(anywhere, anywhere),
        scratch_shapes=[
            pltpu.SemaphoreType.DMA((3, LAYERS, 4)),
            pltpu.SemaphoreType.DMA((3, LAYERS, 4)),
            pltpu.SemaphoreType.DMA((3,)),
        ],
        compiler_params=pltpu.CompilerParams(collective_id=0, has_side_effects=True),
    )(tokens.reshape(2, half, width), table)
    return gathered.reshape(experts, rows, width), tables


def reduce_kernel(part_ref, out_ref, first, second, last, send1, recv1, send2, recv2, send3, recv3):
    z, y, x = grid_place()
    greet()

    def target(k, h, far_first, far_second):
        layer = lax.rem(z + k, LAYERS)
        flip_y, flip_x = (far_second, far_first) if h == 0 else (far_first, far_second)
        return flat_place(layer, 1 - y if flip_y else y, 1 - x if flip_x else x)

    def send(source, slot, partner, send_sem, recv_sem):
        copy = pltpu.make_async_remote_copy(
            src_ref=source, dst_ref=slot, send_sem=send_sem, recv_sem=recv_sem,
            device_id={"expert": partner}, device_id_type=MESH,
        )
        copy.start()
        return copy

    wide = jnp.float32
    order = (2, 1, 3, 0)
    one, two, three = {}, {}, {}

    def open_layer(k):
        for j in range(2):
            for h in range(2):
                one[h, k, j] = send(
                    part_ref.at[target(k, h, True, j == 0), h], first.at[h, k, j],
                    target(0, h, True, False), send1.at[h, k, j], recv1.at[h, k, j],
                )

    def pass_on(k):
        for h in range(2):
            one[h, k, 0].wait_recv()
            mine = part_ref[target(k, h, False, True), h].astype(wide)
            first[h, k, 0] = (mine + first[h, k, 0].astype(wide)).astype(first.dtype)
            two[h, k] = send(
                first.at[h, k, 0], second.at[h, k], target(0, h, False, True),
                send2.at[h, k], recv2.at[h, k],
            )

    def total(k, h):
        one[h, k, 1].wait_recv()
        two[h, k].wait_recv()
        mine = part_ref[target(k, h, False, False), h].astype(wide)
        return mine + first[h, k, 1].astype(wide) + second[h, k].astype(wide)

    def climb(k):
        for h in range(2):
            second[h, k] = total(k, h).astype(second.dtype)
            three[h, k] = send(
                second.at[h, k], last.at[h, k - 1], target(k, h, False, False),
                send3.at[h, k - 1], recv3.at[h, k - 1],
            )

    open_layer(order[0])
    open_layer(order[1])
    pass_on(order[0])
    open_layer(order[2])
    pass_on(order[1])
    climb(order[0])
    open_layer(order[3])
    pass_on(order[2])
    climb(order[1])
    pass_on(order[3])
    climb(order[2])
    for h in range(2):
        value = total(0, h)
        for k in order[:-1]:
            three[h, k].wait_recv()
            value = value + last[h, k - 1].astype(wide)
        out_ref[h] = value.astype(out_ref.dtype)
    for copy in list(one.values()) + list(two.values()) + list(three.values()):
        copy.wait_send()


def reduce_rows(parts):
    experts, rows, width = parts.shape
    half = rows // 2
    inside = pl.BlockSpec(memory_space=pltpu.VMEM)
    dma = pltpu.SemaphoreType.DMA
    mixed = pl.pallas_call(
        reduce_kernel,
        out_shape=jax.ShapeDtypeStruct((2, half, width), parts.dtype),
        in_specs=[inside],
        out_specs=inside,
        scratch_shapes=[
            pltpu.VMEM((2, LAYERS, 2, half, width), parts.dtype),
            pltpu.VMEM((2, LAYERS, half, width), parts.dtype),
            pltpu.VMEM((2, LAYERS - 1, half, width), parts.dtype),
            dma((2, LAYERS, 2)), dma((2, LAYERS, 2)),
            dma((2, LAYERS)), dma((2, LAYERS)),
            dma((2, LAYERS - 1)), dma((2, LAYERS - 1)),
        ],
        compiler_params=pltpu.CompilerParams(
            collective_id=1, has_side_effects=True, vmem_limit_bytes=40 * 1024 * 1024
        ),
    )(parts.reshape(experts, 2, half, width))
    return mixed.reshape(rows, width)


def tree_body(tokens, expert_ids, combine_weights, w_gate, w_up, w_down):
    experts = lax.axis_size("expert")
    tok_rows, model_width = tokens.shape
    top_count = expert_ids.shape[1]
    capacity = min(tok_rows, 5 * tok_rows * top_count // (4 * experts))
    slot_count = experts * capacity
    out_width = w_down.shape[2]
    width_share = model_width // SIDE
    expert_iota = lax.broadcasted_iota(jnp.int32, (1, experts, 1), 1)
    chosen = expert_ids.T[:, None, :] == expert_iota
    table = jnp.sum(jnp.where(chosen, combine_weights.T[:, None, :], 0.0), axis=0)
    place = lax.axis_index("pipe")
    tok_share = lax.dynamic_slice_in_dim(tokens, place * width_share, width_share, 1)
    gathered, tables = gather_rows(tok_share, table)
    weights = lax.dynamic_index_in_dim(tables, lax.axis_index("expert"), 1, keepdims=False)
    named = weights > 0.0
    before = lax.broadcasted_iota(jnp.int32, (tok_rows, tok_rows), 0)
    before = before < lax.broadcasted_iota(jnp.int32, (tok_rows, tok_rows), 1)
    rank = jnp.dot(named.astype(jnp.bfloat16), before.astype(jnp.bfloat16), preferred_element_type=jnp.float32)
    slot = jnp.where(named, rank.astype(jnp.int32), -1)
    marks = slot[:, None, :] == lax.broadcasted_iota(jnp.int32, (1, capacity, 1), 1)
    row_weight = jnp.sum(jnp.where(marks, weights[:, None, :], 0.0), axis=2)
    marks = marks.astype(jnp.bfloat16)
    rows = jnp.einsum("gct,gtd->gcd", marks, gathered, preferred_element_type=jnp.float32)
    rows = rows.astype(jnp.bfloat16).reshape(slot_count, width_share)
    gate_acc, up_acc = split_dots(rows, [w_gate[0], w_up[0]])
    hidden_rows = (jax.nn.silu(gate_acc) * up_acc).astype(jnp.bfloat16)
    (outputs,) = split_dots(hidden_rows, [w_down[0]])
    outputs = (outputs * row_weight.reshape(slot_count, 1)).astype(jnp.bfloat16)
    outputs = outputs.reshape(experts, capacity, out_width)
    parts = jnp.einsum("gct,gcd->gtd", marks, outputs, preferred_element_type=jnp.float32)
    return reduce_rows(parts.astype(jnp.bfloat16))


def split_dots(mine, weights):
    place = lax.axis_index("pipe")
    other = lax.ppermute(mine, "pipe", [(0, 1), (1, 0)])
    share = mine.shape[1]
    totals = []
    for weight in weights:
        own = lax.dynamic_slice_in_dim(weight, place * share, share, 0)
        far = lax.dynamic_slice_in_dim(weight, (1 - place) * share, share, 0)
        total = jnp.dot(mine, own, preferred_element_type=jnp.float32)
        totals.append(total + jnp.dot(other, far, preferred_element_type=jnp.float32))
    return totals


def body(tokens, expert_ids, combine_weights, w_gate, w_up, w_down):
    experts = lax.axis_size("expert")
    tok_rows, model_width = tokens.shape
    top_count = expert_ids.shape[1]
    capacity = min(tok_rows, 5 * tok_rows * top_count // (4 * experts))
    slot_count = experts * capacity
    out_width = w_down.shape[2]
    expert_iota = lax.broadcasted_iota(jnp.int32, (1, 1, experts), 2)
    chosen = (expert_ids[:, :, None] == expert_iota).astype(jnp.int32)
    expert_hits = jnp.sum(chosen, axis=1)
    rank_table = jnp.cumsum(expert_hits, axis=0) - expert_hits
    slot_rank = jnp.sum(chosen * rank_table[:, None, :], axis=2)
    target = expert_ids * capacity + slot_rank
    slot_iota = lax.broadcasted_iota(jnp.int32, (1, 1, slot_count), 2)
    slot_marks = target[:, :, None] == slot_iota
    placing = jnp.any(slot_marks, axis=1).astype(jnp.bfloat16)
    blend_table = jnp.sum(jnp.where(slot_marks, combine_weights[:, :, None], 0.0), axis=1)
    pipes = lax.axis_size("pipe")
    place = lax.axis_index("pipe")
    width_share = model_width // pipes
    tok_share = lax.dynamic_slice_in_dim(tokens, place * width_share, width_share, 1)
    packed = jnp.einsum("ts,td->sd", placing, tok_share, preferred_element_type=jnp.float32)
    packed = packed.astype(jnp.bfloat16).reshape(experts, capacity, width_share)
    received = lax.all_to_all(packed, "expert", split_axis=0, concat_axis=0, tiled=True)
    rows = received.reshape(slot_count, width_share)
    if pipes == 2:
        gate_acc, up_acc = split_dots(rows, [w_gate[0], w_up[0]])
    else:
        rows = lax.all_gather(rows, "pipe", axis=1, tiled=True)
        gate_acc = jnp.dot(rows, w_gate[0], preferred_element_type=jnp.float32)
        up_acc = jnp.dot(rows, w_up[0], preferred_element_type=jnp.float32)
    hidden_rows = (jax.nn.silu(gate_acc) * up_acc).astype(jnp.bfloat16)
    if pipes == 2:
        (outputs,) = split_dots(hidden_rows, [w_down[0]])
    else:
        outputs = jnp.dot(
            lax.all_gather(hidden_rows, "pipe", axis=1, tiled=True),
            w_down[0],
            preferred_element_type=jnp.float32,
        )
    outgoing = outputs.astype(jnp.bfloat16).reshape(experts, capacity, out_width)
    returned_rows = lax.all_to_all(outgoing, "expert", split_axis=0, concat_axis=0, tiled=True)
    mixture = jnp.dot(
        blend_table,
        returned_rows.reshape(slot_count, out_width).astype(jnp.float32),
        precision=lax.Precision.HIGHEST,
        preferred_element_type=jnp.float32,
    )
    return mixture.astype(jnp.bfloat16)


def solution(mesh):
    placed = (
        P("expert", None),
        P("expert", None),
        P("expert", None),
        P("expert", None, "pipe"),
        P("expert", None, "pipe"),
        P("expert", None, "pipe"),
    )
    tree = mesh.shape["pipe"] == SIDE and mesh.shape["expert"] == LAYERS * SIDE * SIDE
    return jax.shard_map(
        tree_body if tree else body, mesh=mesh, in_specs=placed, out_specs=P("expert", "pipe"), check_vma=False
    )
```

```python
import jax
import jax.numpy as jnp
from jax import lax
from jax.experimental import pallas as pl
from jax.experimental.pallas import tpu as pltpu
from jax.sharding import PartitionSpec as P

LAYERS, SIDE = 4, 2
MESH = pl.DeviceIdType.MESH


def grid_place():
    me = lax.axis_index("expert")
    return me // 4, lax.rem(me // 2, 2), lax.rem(me, 2)


def flat_place(z, y, x):
    return z * 4 + y * 2 + x


def greet():
    z, y, x = grid_place()
    barrier = pltpu.get_barrier_semaphore()
    partners = [flat_place(lax.rem(z + k, LAYERS), y, x) for k in range(1, LAYERS)]
    partners += [flat_place(z, 1 - y, x), flat_place(z, y, 1 - x)]
    for partner in partners:
        pl.semaphore_signal(barrier, inc=1, device_id={"expert": partner}, device_id_type=MESH)
    pl.semaphore_wait(barrier, len(partners))


def gather_kernel(tok_ref, table_ref, out_ref, tables_ref, send_sem, recv_sem, local_sem):
    z, y, x = grid_place()
    me = flat_place(z, y, x)
    greet()
    own = [tok_ref.at[0], tok_ref.at[1], table_ref]
    slots = [lambda e: out_ref.at[e, 0], lambda e: out_ref.at[e, 1], lambda e: tables_ref.at[e]]
    hops = [
        (flat_place(z, 1 - y, x), flat_place(z, y, 1 - x)),
        (flat_place(z, y, 1 - x), flat_place(z, 1 - y, x)),
        (flat_place(z, 1 - y, x), flat_place(z, y, 1 - x)),
    ]
    kept = [pltpu.make_async_copy(own[j], slots[j](me), local_sem.at[j]) for j in range(3)]
    started = []

    def send(source, slot, partner, j, k, step):
        copy = pltpu.make_async_remote_copy(
            src_ref=source, dst_ref=slot, send_sem=send_sem.at[j, k, step],
            recv_sem=recv_sem.at[j, k, step], device_id={"expert": partner}, device_id_type=MESH,
        )
        copy.start()
        started.append(copy)
        return copy

    order = (2, 0, 1)
    along, near = {}, {}

    def climb(k):
        for j in order:
            along[j, k] = send(own[j], slots[j](me), flat_place(lax.rem(z + k, LAYERS), y, x), j, k, 0)

    def spread(k):
        origin = flat_place(lax.rem(z - k + LAYERS, LAYERS), y, x)
        for j in order:
            source = slots[j](origin) if k else own[j]
            near[j, k] = send(source, slots[j](origin), hops[j][0], j, k, 1)
            send(source, slots[j](origin), hops[j][1], j, k, 2)

    def forward(k):
        layer = lax.rem(z - k + LAYERS, LAYERS)
        for j in order:
            origin = flat_place(layer, y, 1 - x) if j == 1 else flat_place(layer, 1 - y, x)
            near[j, k].wait_recv()
            send(slots[j](origin), slots[j](origin), hops[j][1], j, k, 3)

    climb(1)
    climb(3)
    spread(0)
    for copy in kept:
        copy.start()
    previous = 0
    for k, later in ((1, None), (3, 2), (2, None)):
        for j in order:
            along[j, k].wait_recv()
        if later:
            climb(later)
        spread(k)
        forward(previous)
        previous = k
    forward(previous)
    for copy in kept:
        copy.wait()
    for copy in started:
        copy.wait_send()
    waited = list(along.values()) + list(near.values())
    for copy in started:
        if not any(copy is other for other in waited):
            copy.wait_recv()


def gather_rows(tokens, table):
    rows, width = tokens.shape
    experts = lax.axis_size("expert")
    half = rows // 2
    anywhere = pl.BlockSpec(memory_space=pl.ANY)
    gathered, tables = pl.pallas_call(
        gather_kernel,
        out_shape=(
            jax.ShapeDtypeStruct((experts, 2, half, width), tokens.dtype),
            jax.ShapeDtypeStruct((experts,) + table.shape, table.dtype),
        ),
        in_specs=[anywhere, anywhere],
        out_specs=(anywhere, anywhere),
        scratch_shapes=[
            pltpu.SemaphoreType.DMA((3, LAYERS, 4)),
            pltpu.SemaphoreType.DMA((3, LAYERS, 4)),
            pltpu.SemaphoreType.DMA((3,)),
        ],
        compiler_params=pltpu.CompilerParams(collective_id=0, has_side_effects=True),
    )(tokens.reshape(2, half, width), table)
    return gathered.reshape(experts, rows, width), tables


def reduce_kernel(part_ref, out_ref, first, second, last, send1, recv1, send2, recv2, send3, recv3):
    z, y, x = grid_place()
    greet()

    def target(k, h, far_first, far_second):
        layer = lax.rem(z + k, LAYERS)
        flip_y, flip_x = (far_second, far_first) if h == 0 else (far_first, far_second)
        return flat_place(layer, 1 - y if flip_y else y, 1 - x if flip_x else x)

    def send(source, slot, partner, send_sem, recv_sem):
        copy = pltpu.make_async_remote_copy(
            src_ref=source, dst_ref=slot, send_sem=send_sem, recv_sem=recv_sem,
            device_id={"expert": partner}, device_id_type=MESH,
        )
        copy.start()
        return copy

    wide = jnp.float32
    order = (2, 1, 3, 0)
    one, two, three = {}, {}, {}

    def open_layer(k):
        for j in range(2):
            for h in range(2):
                one[h, k, j] = send(
                    part_ref.at[target(k, h, True, j == 0), h], first.at[h, k, j],
                    target(0, h, True, False), send1.at[h, k, j], recv1.at[h, k, j],
                )

    def pass_on(k):
        for h in range(2):
            one[h, k, 0].wait_recv()
            mine = part_ref[target(k, h, False, True), h].astype(wide)
            first[h, k, 0] = (mine + first[h, k, 0].astype(wide)).astype(first.dtype)
            two[h, k] = send(
                first.at[h, k, 0], second.at[h, k], target(0, h, False, True),
                send2.at[h, k], recv2.at[h, k],
            )

    def total(k, h):
        one[h, k, 1].wait_recv()
        two[h, k].wait_recv()
        mine = part_ref[target(k, h, False, False), h].astype(wide)
        return mine + first[h, k, 1].astype(wide) + second[h, k].astype(wide)

    def climb(k):
        for h in range(2):
            second[h, k] = total(k, h).astype(second.dtype)
            three[h, k] = send(
                second.at[h, k], last.at[h, k - 1], target(k, h, False, False),
                send3.at[h, k - 1], recv3.at[h, k - 1],
            )

    open_layer(order[0])
    open_layer(order[1])
    pass_on(order[0])
    open_layer(order[2])
    pass_on(order[1])
    climb(order[0])
    open_layer(order[3])
    pass_on(order[2])
    climb(order[1])
    pass_on(order[3])
    climb(order[2])
    for h in range(2):
        value = total(0, h)
        for k in order[:-1]:
            three[h, k].wait_recv()
            value = value + last[h, k - 1].astype(wide)
        out_ref[h] = value.astype(out_ref.dtype)
    for copy in list(one.values()) + list(two.values()) + list(three.values()):
        copy.wait_send()


def reduce_rows(parts):
    experts, rows, width = parts.shape
    half = rows // 2
    inside = pl.BlockSpec(memory_space=pltpu.VMEM)
    dma = pltpu.SemaphoreType.DMA
    mixed = pl.pallas_call(
        reduce_kernel,
        out_shape=jax.ShapeDtypeStruct((2, half, width), parts.dtype),
        in_specs=[inside],
        out_specs=inside,
        scratch_shapes=[
            pltpu.VMEM((2, LAYERS, 2, half, width), parts.dtype),
            pltpu.VMEM((2, LAYERS, half, width), parts.dtype),
            pltpu.VMEM((2, LAYERS - 1, half, width), parts.dtype),
            dma((2, LAYERS, 2)), dma((2, LAYERS, 2)),
            dma((2, LAYERS)), dma((2, LAYERS)),
            dma((2, LAYERS - 1)), dma((2, LAYERS - 1)),
        ],
        compiler_params=pltpu.CompilerParams(
            collective_id=1, has_side_effects=True, vmem_limit_bytes=40 * 1024 * 1024
        ),
    )(parts.reshape(experts, 2, half, width))
    return mixed.reshape(rows, width)


def tree_body(tokens, expert_ids, combine_weights, w_gate, w_up, w_down):
    experts = lax.axis_size("expert")
    tok_rows, model_width = tokens.shape
    top_count = expert_ids.shape[1]
    capacity = min(tok_rows, 5 * tok_rows * top_count // (4 * experts))
    slot_count = experts * capacity
    out_width = w_down.shape[2]
    width_share = model_width // SIDE
    expert_iota = lax.broadcasted_iota(jnp.int32, (1, experts, 1), 1)
    chosen = expert_ids.T[:, None, :] == expert_iota
    table = jnp.sum(jnp.where(chosen, combine_weights.T[:, None, :], 0.0), axis=0)
    place = lax.axis_index("pipe")
    tok_share = lax.dynamic_slice_in_dim(tokens, place * width_share, width_share, 1)
    gathered, tables = gather_rows(tok_share, table)
    weights = lax.dynamic_index_in_dim(tables, lax.axis_index("expert"), 1, keepdims=False)
    named = weights > 0.0
    before = lax.broadcasted_iota(jnp.int32, (tok_rows, tok_rows), 0)
    before = before < lax.broadcasted_iota(jnp.int32, (tok_rows, tok_rows), 1)
    rank = jnp.dot(named.astype(jnp.bfloat16), before.astype(jnp.bfloat16), preferred_element_type=jnp.float32)
    slot = jnp.where(named, rank.astype(jnp.int32), -1)
    marks = slot[:, None, :] == lax.broadcasted_iota(jnp.int32, (1, capacity, 1), 1)
    row_weight = jnp.sum(jnp.where(marks, weights[:, None, :], 0.0), axis=2)
    marks = marks.astype(jnp.bfloat16)
    rows = jnp.einsum("gct,gtd->gcd", marks, gathered, preferred_element_type=jnp.float32)
    rows = rows.astype(jnp.bfloat16).reshape(slot_count, width_share)
    gate_acc, up_acc = split_dots(rows, [w_gate[0], w_up[0]])
    hidden_rows = (jax.nn.silu(gate_acc) * up_acc).astype(jnp.bfloat16)
    (outputs,) = split_dots(hidden_rows, [w_down[0]])
    outputs = (outputs * row_weight.reshape(slot_count, 1)).astype(jnp.bfloat16)
    outputs = outputs.reshape(experts, capacity, out_width)
    parts = jnp.einsum("gct,gcd->gtd", marks, outputs, preferred_element_type=jnp.float32)
    return reduce_rows(parts.astype(jnp.bfloat16))


def split_dots(mine, weights):
    place = lax.axis_index("pipe")
    other = lax.ppermute(mine, "pipe", [(0, 1), (1, 0)])
    share = mine.shape[1]
    totals = []
    for weight in weights:
        own = lax.dynamic_slice_in_dim(weight, place * share, share, 0)
        far = lax.dynamic_slice_in_dim(weight, (1 - place) * share, share, 0)
        total = jnp.dot(mine, own, preferred_element_type=jnp.float32)
        totals.append(total + jnp.dot(other, far, preferred_element_type=jnp.float32))
    return totals


def body(tokens, expert_ids, combine_weights, w_gate, w_up, w_down):
    experts = lax.axis_size("expert")
    tok_rows, model_width = tokens.shape
    top_count = expert_ids.shape[1]
    capacity = min(tok_rows, 5 * tok_rows * top_count // (4 * experts))
    slot_count = experts * capacity
    out_width = w_down.shape[2]
    expert_iota = lax.broadcasted_iota(jnp.int32, (1, 1, experts), 2)
    chosen = (expert_ids[:, :, None] == expert_iota).astype(jnp.int32)
    expert_hits = jnp.sum(chosen, axis=1)
    rank_table = jnp.cumsum(expert_hits, axis=0) - expert_hits
    slot_rank = jnp.sum(chosen * rank_table[:, None, :], axis=2)
    target = expert_ids * capacity + slot_rank
    slot_iota = lax.broadcasted_iota(jnp.int32, (1, 1, slot_count), 2)
    slot_marks = target[:, :, None] == slot_iota
    placing = jnp.any(slot_marks, axis=1).astype(jnp.bfloat16)
    blend_table = jnp.sum(jnp.where(slot_marks, combine_weights[:, :, None], 0.0), axis=1)
    pipes = lax.axis_size("pipe")
    place = lax.axis_index("pipe")
    width_share = model_width // pipes
    tok_share = lax.dynamic_slice_in_dim(tokens, place * width_share, width_share, 1)
    packed = jnp.einsum("ts,td->sd", placing, tok_share, preferred_element_type=jnp.float32)
    packed = packed.astype(jnp.bfloat16).reshape(experts, capacity, width_share)
    received = lax.all_to_all(packed, "expert", split_axis=0, concat_axis=0, tiled=True)
    rows = received.reshape(slot_count, width_share)
    if pipes == 2:
        gate_acc, up_acc = split_dots(rows, [w_gate[0], w_up[0]])
    else:
        rows = lax.all_gather(rows, "pipe", axis=1, tiled=True)
        gate_acc = jnp.dot(rows, w_gate[0], preferred_element_type=jnp.float32)
        up_acc = jnp.dot(rows, w_up[0], preferred_element_type=jnp.float32)
    hidden_rows = (jax.nn.silu(gate_acc) * up_acc).astype(jnp.bfloat16)
    if pipes == 2:
        (outputs,) = split_dots(hidden_rows, [w_down[0]])
    else:
        outputs = jnp.dot(
            lax.all_gather(hidden_rows, "pipe", axis=1, tiled=True),
            w_down[0],
            preferred_element_type=jnp.float32,
        )
    outgoing = outputs.astype(jnp.bfloat16).reshape(experts, capacity, out_width)
    returned_rows = lax.all_to_all(outgoing, "expert", split_axis=0, concat_axis=0, tiled=True)
    mixture = jnp.dot(
        blend_table,
        returned_rows.reshape(slot_count, out_width).astype(jnp.float32),
        precision=lax.Precision.HIGHEST,
        preferred_element_type=jnp.float32,
    )
    return mixture.astype(jnp.bfloat16)


def solution(mesh):
    placed = (
        P("expert", None),
        P("expert", None),
        P("expert", None),
        P("expert", None, "pipe"),
        P("expert", None, "pipe"),
        P("expert", None, "pipe"),
    )
    tree = mesh.shape["pipe"] == SIDE and mesh.shape["expert"] == LAYERS * SIDE * SIDE
    return jax.shard_map(
        tree_body if tree else body, mesh=mesh, in_specs=placed, out_specs=P("expert", "pipe"), check_vma=False
    )
```
